128 devices in a mesh: cols: 16 (over x_hi, y, core), rows: 8 (over z, x_lo).
Axes of the slice: x: 4 (x_hi: 2, x_lo: 2; x = x_hi * 2 + x_lo), y: 4, z: 4, core: 2. Of those that a mesh axis runs over, the one named last changes fastest.
Arguments:
- weight: float32 [8192, 13, 2048], P('rows', None, 'cols'), may hold values from -6 to 6
- factor_rows: bfloat16 [1024, 13, 2048], P('rows', None, 'cols'), may hold values from -0.1875 to 0.1875
- diag_inverse: float32 [8, 128, 128], replicated, may hold values from -1 to 2, as said below
- keep_codes: int32 [8192, 256], P('rows'), may hold values from 0 to 5
- block_order: int32 [8], replicated, may hold values from 0 to 7, each once
Outputs:
- pruned: float32 [8192, 13, 2048], P('rows', None, 'cols')
The draws below stay inside these ranges and needn't reach their ends.
Inputs may be any that keep to these rules, and one draw needn't show every extreme that they name: `block_order`: each entry of 0 to 7 appears once. `diag_inverse`: upper triangular with diagonal entries of 1 to 2.
All inputs are finite; a program needn't handle non-finite values.
Results may differ from the reference program's by a relative error of at most 0.0028.
Values may be sent and summed in bfloat16 or wider, within the bound.
No kernel may reach another device: no remote copies, remote signals or barrier semaphores. Data moves between devices by JAX's collectives and lax.ppermute only.
A program may use at most 128 MiB of HBM per device.

```python
import jax
import jax.numpy as jnp
import numpy as np
from jax import lax

FF = 26624
BS = 128
BLOCKS = 8
R = 8192
LAPS = 13
N_COLS = 16


def draw_diag_inverse(key, part):
    first, second = jax.random.split(jax.random.fold_in(key, 11), 2)
    diagonal = jax.random.uniform(first, (BLOCKS, BS), jnp.float32, 1.0, 2.0)
    others = 0.4 * jax.random.normal(second, (BLOCKS, BS, BS), jnp.float32) / jnp.sqrt(jnp.float32(BS))
    upper = jnp.triu(others, 1)
    return upper + diagonal[:, :, None] * jnp.eye(BS, dtype=jnp.float32)[None, :, :]


def set_ends(entries, own_key, smallest, high):
    spot = [jax.random.randint(jax.random.fold_in(own_key, axis), (), 0, length) for axis, length in enumerate(entries.shape)]
    widest = entries.shape.index(max(entries.shape))
    beside = spot[:widest] + [(spot[widest] + 1) % entries.shape[widest]] + spot[widest + 1:]
    return entries.at[tuple(spot)].set(smallest).at[tuple(beside)].set(high)


def shard_levels(key, shape, pieces, low, high):
    def one(position, blocks):
        steps = jax.random.uniform(jax.random.fold_in(jax.random.fold_in(key, 6), position), (blocks,), jnp.float32, low / len(pieces), high / len(pieces))
        return jnp.repeat(jnp.exp(steps), shape[position] // blocks).reshape((-1,) + (1,) * (len(shape) - position - 1))

    loudness = one(*pieces[0])
    for cut in pieces[1:]:
        loudness = loudness * one(*cut)
    return loudness


def gaussian(stream_key, dims, scale, bound, pieces=(), kind=jnp.bfloat16):
    drawn = jax.random.normal(stream_key, dims, jnp.float32) * scale
    if len(pieces) > 0:
        drawn = shard_levels(stream_key, dims, pieces, -0.22, 0.18) * drawn
    return jnp.clip(drawn, min=-bound, max=bound).astype(kind)


def setup_inputs(seed: int = 0) -> dict:
    key_of = jax.random.split(jax.random.key(seed), 6)
    weight = gaussian(key_of[0], (R, LAPS, N_COLS * BS), 1.0, 6.0, ((0, 8), (2, 16)), jnp.float32)
    factor_rows = gaussian(key_of[1], (BLOCKS * BS, LAPS, N_COLS * BS), (BLOCKS * BS) ** -0.5, 0.1875, ((0, 8), (2, 16)))
    diag_inverse = draw_diag_inverse(jax.random.fold_in(key_of[5], 71), 0)
    keep_codes = set_ends(jax.random.randint(key_of[3], (R, BLOCKS * 32), 0, 6), jax.random.fold_in(key_of[3], 1), 0, 5).astype(jnp.int32)
    block_order = jax.random.permutation(key_of[4], BLOCKS).astype(jnp.int32)
    return dict(weight=weight, factor_rows=factor_rows, diag_inverse=diag_inverse, keep_codes=keep_codes, block_order=block_order)


pair_table = np.array([[1, 1, 0, 0], [1, 0, 1, 0], [1, 0, 0, 1], [0, 1, 1, 0], [0, 1, 0, 1], [0, 0, 1, 1]], dtype=np.float32)


def decode(codes):
    onehot = (codes[:, :, None] == jnp.arange(6, dtype=jnp.int32)).astype(jnp.float32)
    kept_mask = jnp.einsum("rgo,ok->rgk", onehot, jnp.asarray(pair_table, dtype=jnp.float32))
    return kept_mask.reshape(codes.shape[0], -1)


def reference(weight, factor_rows, diag_inverse, keep_codes, block_order):
    row_count = weight.shape[0]
    matrix = weight.reshape(row_count, FF)
    factor = factor_rows.reshape(BLOCKS * BS, FF)
    column_block = jnp.arange(FF, dtype=jnp.int32) // BS
    finished = jnp.zeros((FF // BS,), dtype=bool)
    for step_index in range(BLOCKS):
        block_now = block_order[step_index].astype(jnp.int32)
        col_start = (block_now * BS).astype(jnp.int32)
        block_vals = lax.dynamic_slice_in_dim(matrix, col_start, BS, 1)
        kept_mask = decode(lax.dynamic_slice_in_dim(keep_codes, (block_now * 32).astype(jnp.int32), 32, 1))
        errors_bf = jnp.dot(block_vals * (1.0 - kept_mask), diag_inverse[block_now], precision=lax.Precision.HIGHEST, preferred_element_type=jnp.float32).astype(jnp.bfloat16)
        finished = finished.at[block_now].set(True)
        factor_tile = lax.dynamic_slice_in_dim(factor, col_start, BS, 0)
        update_term = jnp.dot(errors_bf, factor_tile, preferred_element_type=jnp.float32)
        pending = jnp.logical_not(finished[column_block])
        matrix = jnp.where(pending[None, :], matrix - update_term, matrix)
        matrix = lax.dynamic_update_slice_in_dim(matrix, block_vals * kept_mask, col_start, 1)
    return matrix.reshape(weight.shape)
```

```python
import functools

import jax
import jax.numpy as jnp
from jax import lax
from jax.experimental import pallas as pl
from jax.experimental.pallas import tpu as pltpu
from jax.sharding import PartitionSpec as P


BLOCKS = 8
T = 128
PACK_VMEM = 16 << 20
CHAIN_VMEM = 24 << 20
UPDATE_VMEM = 24 << 20
CORE, BLOCK, Z, XL, Y = range(5)
bf16 = jnp.bfloat16
f32 = jnp.float32


def lanes(shape):
    return lax.broadcasted_iota(jnp.int32, shape, len(shape) - 1)


def by_lane(values, shape):
    place = lanes(shape) & 3
    out = jnp.full(shape, values[0], jnp.int32)
    for p in range(1, 4):
        out = jnp.where(place == p, values[p], out)
    return out


def lane_codes(codes, block):
    return jnp.take_along_axis(codes, (block & 3) * (T // 4) + lanes(codes.shape) // 4, axis=1)


def pruned_columns(code):
    return ((by_lane((56, 38, 21, 11), code.shape) >> code) & 1) == 1


def pack(values, code):
    half = values.shape[0] // 2
    shift = (by_lane((22, 410, 22, 410), code.shape) >> (2 * code)) & 3
    va, vb, sa, sb = values[:half], values[half:], shift[:half], shift[half:]
    a = jnp.where(sa == 0, va, jnp.where(sa == 1, pltpu.roll(va, T - 1, 1), pltpu.roll(va, T - 2, 1)))
    b = jnp.where(sb == 2, vb, jnp.where(sb == 1, pltpu.roll(vb, 1, 1), pltpu.roll(vb, 2, 1)))
    return jnp.where((lanes(a.shape) & 3) < 2, a, b)


def unpack(packed, code_a, code_b):
    table = by_lane((0, 341, 1366, 2730), code_a.shape)
    sa, sb = (table >> (2 * code_a)) & 3, (table >> (2 * code_b)) & 3
    a = jnp.where(sa == 0, packed, jnp.where(sa == 1, pltpu.roll(packed, 1, 1), pltpu.roll(packed, 2, 1)))
    b = jnp.where(sb == 2, packed, jnp.where(sb == 1, pltpu.roll(packed, T - 1, 1), pltpu.roll(packed, T - 2, 1)))
    return a, b


def half_rows(meta, own_half, half):
    return pl.ds(pl.multiple_of((meta[CORE] if own_half else 1 - meta[CORE]) * half, half), half)


def pack_kernel(meta, w_ref, codes_ref, packed_ref, code_ref):
    rows = w_ref.shape[1]
    half = rows // 2
    for h in range(2):
        at = slice(h * half, (h + 1) * half)
        code = lane_codes(codes_ref[at, :], meta[BLOCK])
        code_ref[at, :] = code
        packed_ref[h * half // 2 : (h + 1) * half // 2, :] = pack(w_ref[0, at, :], code)


def chain_kernel(meta, order, *refs):
    codes_hbm, diag_hbm, w_hbm = refs[:3]
    packed_refs, own_refs, other_refs = refs[3:11], refs[11:15], refs[15:19]
    e_ref, w_near, done, packed, factor, codes_ref, diag_ref, arrived = refs[19:]
    mine = half_rows(meta, True, e_ref.shape[0])
    fetches = [
        pltpu.make_async_copy(codes_hbm.at[mine], codes_ref, arrived.at[0]),
        pltpu.make_async_copy(diag_hbm, diag_ref, arrived.at[1]),
        pltpu.make_async_copy(w_hbm.at[:, mine], w_near, arrived.at[2]),
    ]
    for fetch in fetches:
        fetch.start()
    quarter = packed.shape[1]
    mine = pl.ds(pl.multiple_of(meta[CORE] * quarter, quarter), quarter)
    for i in range(4):
        packed[2 * i] = packed_refs[i][mine, :]
        packed[2 * i + 1] = packed_refs[4 + i][mine, :]
        for k in range(BLOCKS):
            at = slice(k * T, (k + 1) * T)
            factor[2 * i, k] = own_refs[i][at, :]
            factor[2 * i + 1, k] = other_refs[i][at, :]
    rows = e_ref.shape[0]
    half = rows // 2
    fetches[0].wait()
    fetches[1].wait()
    row_places = []
    for s in range(BLOCKS):
        b = order[s]
        row_places.append(2 * ((b // 2 - meta[Z]) & 3) + ((b & 1) ^ meta[XL]))
        c_at = 2 * ((b // 2 - meta[Y]) & 3) + ((b & 1) ^ meta[CORE])
        k_at = pl.ds(pl.multiple_of(row_places[s] * T, T), T)
        diag = diag_ref[b]
        high = diag.astype(bf16)
        low = (diag - high.astype(f32)).astype(bf16)
        split = jnp.concatenate([jnp.concatenate([high, low], 1)] * 2, 0)
        code = lane_codes(codes_ref[:, pl.ds(pl.multiple_of((b // 4) * T, T), T)], b)
        pruned = pruned_columns(code)
        values = unpack(packed[c_at], code[:half], code[half:])
        if s:
            tiles = jnp.concatenate([factor[c_at, k] for k in row_places[:s]], 0)
        for h in range(2):
            at = slice(h * half, (h + 1) * half)
            now = values[h]
            if s:
                now = now - jnp.dot(done[at, : s * T], tiles, preferred_element_type=f32)
            now = jnp.where(pruned[at], now, 0.0)
            hi = now.astype(bf16)
            lo = (now - hi.astype(f32)).astype(bf16)
            both = jnp.dot(jnp.concatenate([hi, lo], 1), split, preferred_element_type=f32)
            e = (both[:, :T] + both[:, T:]).astype(bf16)
            done[at, s * T : (s + 1) * T] = e
            e_ref[at, k_at] = e
    fetches[2].wait()


def update_kernel(own_half, meta, order, w_ref, code_ref, e_ref, *refs):
    f_refs = refs[:BLOCKS]
    if own_half:
        w_hbm, out_ref, w_next, buffer, sent, takes, arrived = refs[BLOCKS:]
    else:
        _, out_ref, buffer, sent, takes = refs[BLOCKS:]
    laps, half = w_ref.shape[0], e_ref.shape[0]
    block = meta[BLOCK]
    rows = half_rows(meta, own_half, half)
    if own_half:
        fetch = pltpu.make_async_copy(w_hbm.at[:, half_rows(meta, False, half)], w_next, arrived)
        fetch.start()

    step_of = [sum(s * (order[s] == b).astype(jnp.int32) for s in range(1, BLOCKS)) for b in range(BLOCKS)]
    mine = sum(step_of[b] * (block == b).astype(jnp.int32) for b in range(BLOCKS))
    for b in range(BLOCKS):
        place = 2 * ((b // 2 - meta[Z]) & 3) + ((b & 1) ^ meta[XL])
        takes[place] = jnp.logical_or(step_of[b] < mine, block >= BLOCKS).astype(jnp.int32)

    def send(i, count=2):
        at = pl.ds(2 * i, count)
        return pltpu.make_async_copy(buffer.at[at], out_ref.at[at, rows], sent.at[i])

    @pl.loop(0, pl.cdiv(laps, 2))
    def _(i):
        late = jnp.minimum(2 * i + 1, laps - 1)
        parts = []
        for j, f_ref in enumerate(f_refs):
            drop = jnp.logical_and(i == 0, takes[j] == 0)
            f0 = jnp.where(drop, 0.0, f_ref[2 * i].astype(f32)).astype(bf16)
            parts.append(jnp.concatenate([f0, f_ref[late]], 1))
        product = jnp.dot(e_ref[...], jnp.concatenate(parts, 0), preferred_element_type=f32)
        buffer[2 * i] = w_ref[2 * i] - product[:, :T]
        buffer[2 * i + 1] = w_ref[late] - product[:, T:]

        @pl.when(jnp.logical_and(i == 0, block < BLOCKS))
        def _():
            buffer[0] = jnp.where(pruned_columns(code_ref[rows, :]), 0.0, buffer[0])

        @pl.when(2 * i + 1 < laps)
        def _():
            send(i).start()

    if laps % 2:
        send(laps // 2, 1).start()
    for i in range(laps // 2):
        send(i).wait()
    if laps % 2:
        send(laps // 2, 1).wait()
    if own_half:
        fetch.wait()


def body(weight, factor_rows, diag_inverse, keep_codes, block_order):
    cols, rows = lax.axis_size("cols"), lax.axis_size("rows")
    c, r = lax.axis_index("cols"), lax.axis_index("rows")
    x_hi, y, core = c // 8, (c // 2) % 4, c % 2
    z, xl = r // 2, r % 2
    near = x_hi == 0
    w = pltpu.with_memory_space_constraint(jnp.transpose(weight, (1, 0, 2)), pltpu.HBM)
    keep_codes = pltpu.with_memory_space_constraint(keep_codes, pltpu.HBM)
    diag_inverse = pltpu.with_memory_space_constraint(diag_inverse, pltpu.HBM)
    f = jnp.transpose(factor_rows, (1, 0, 2))
    laps, m, _ = w.shape
    half = m // 2

    meta = jnp.stack([core, c, z, xl, y]).astype(jnp.int32)

    def from_core(a):
        return lax.ppermute(a, "cols", [(i ^ 1, i) for i in range(cols)])

    def from_y(a, d):
        return lax.ppermute(a, "cols", [((i & 9) | ((i + 2 * d) & 6), i) for i in range(cols)])

    def from_xl(a):
        return lax.ppermute(a, "rows", [(i ^ 1, i) for i in range(rows)])

    def from_z(a, d):
        return lax.ppermute(a, "rows", [((i + 2 * d) % rows, i) for i in range(rows)])

    f0 = f[0]
    both = ("cols", "rows")
    held = [(i * rows + j, i, j) for i in range(8) for j in range(rows)]
    mine = lax.ppermute(f0, both, [(at, (i + 8) * rows + j) for at, i, j in held])
    next_far = lax.ppermute(f0, both, [(at, (i + 8) * rows + (j ^ 1)) for at, i, j in held])
    next_near = lax.ppermute(f0, both, [(at, i * rows + (j ^ 1)) for at, i, j in held])
    pair = jnp.concatenate([jnp.where(near, f0, mine), jnp.where(near, next_near, next_far)], 0)
    column = jnp.concatenate([pair] + [from_z(pair, d) for d in range(1, 4)], 0)

    packed, code = pl.pallas_call(
        pack_kernel,
        out_shape=[
            jax.ShapeDtypeStruct((half, T), f32),
            jax.ShapeDtypeStruct((m, T), jnp.int32),
        ],
        grid_spec=pltpu.PrefetchScalarGridSpec(
            num_scalar_prefetch=1,
            grid=(1,),
            in_specs=[
                pl.BlockSpec((1, m, T), lambda i, s: (0, 0, 0)),
                pl.BlockSpec((m, T), lambda i, s: (0, jnp.minimum(s[BLOCK] // 4, 1))),
            ],
            out_specs=[pl.BlockSpec((half, T), lambda i, s: (0, 0)), pl.BlockSpec((m, T), lambda i, s: (0, 0))],
        ),
        compiler_params=pltpu.CompilerParams(vmem_limit_bytes=PACK_VMEM),
        cost_estimate=pl.CostEstimate(flops=10**8, bytes_accessed=2 << 20, transcendentals=0),
        name="pack",
    )(meta, w, keep_codes)
    packed = jnp.where(near, packed, lax.ppermute(packed, "cols", [(i, i + 8) for i in range(8)]))

    packed = [packed, from_y(packed, 1), None, from_y(packed, 3)]
    packed[2] = from_y(packed[3], 3)
    packed += [from_core(packed[d]) for d in range(4)]

    columns = [column, from_y(column, 1), None, from_y(column, 3)]
    columns[2] = from_y(columns[1], 1)
    others = [from_core(columns[d]) for d in range(4)]

    f_xl = from_xl(f)
    f_z = {d: from_z(f, d) for d in range(1, 4)}
    f_all = [f, f_xl]
    for d in range(1, 4):
        f_all += [f_z[d], from_xl(f_z[d]) if d == 2 else from_z(f_xl, d)]

    smem = pl.BlockSpec(memory_space=pltpu.SMEM)
    vmem = pl.BlockSpec(memory_space=pltpu.VMEM)
    hbm = pl.BlockSpec(memory_space=pl.ANY)
    w_half = jax.ShapeDtypeStruct((laps, half, T), f32)
    e_own, w_near = pl.pallas_call(
        chain_kernel,
        out_shape=[jax.ShapeDtypeStruct((half, BLOCKS * T), bf16), w_half],
        in_specs=[smem, smem, hbm, hbm, hbm] + [vmem] * 16,
        out_specs=[vmem, vmem],
        scratch_shapes=[
            pltpu.VMEM((half, BLOCKS * T), bf16),
            pltpu.VMEM((BLOCKS, half // 2, T), f32),
            pltpu.VMEM((BLOCKS, BLOCKS, T, T), bf16),
            pltpu.VMEM((half, keep_codes.shape[1]), jnp.int32),
            pltpu.VMEM(diag_inverse.shape, f32),
            pltpu.SemaphoreType.DMA((3,)),
        ],
        compiler_params=pltpu.CompilerParams(vmem_limit_bytes=CHAIN_VMEM),
        cost_estimate=pl.CostEstimate(flops=4 * 10**9, bytes_accessed=8 << 20, transcendentals=0),
        name="chain",
    )(meta, block_order, keep_codes, diag_inverse, w, *packed, *columns, *others)
    e_other = from_core(e_own)

    out = None
    for turn, e in enumerate([e_own, e_other]):
        own_half = turn == 0

        result = pl.pallas_call(
            functools.partial(update_kernel, own_half),
            out_shape=[jax.ShapeDtypeStruct(w.shape, f32)] + [w_half] * own_half,
            in_specs=[smem, smem] + [vmem] * (3 + BLOCKS) + [hbm],
            out_specs=[hbm] + [vmem] * own_half,
            scratch_shapes=[
                pltpu.VMEM((laps + laps % 2, half, T), f32),
                pltpu.SemaphoreType.DMA((laps // 2 + laps % 2,)),
                pltpu.SMEM((BLOCKS,), jnp.int32),
            ]
            + [pltpu.SemaphoreType.DMA(())] * own_half,
            input_output_aliases={} if own_half else {5 + BLOCKS: 0},
            compiler_params=pltpu.CompilerParams(vmem_limit_bytes=UPDATE_VMEM),
            cost_estimate=pl.CostEstimate(flops=2 * 10**9, bytes_accessed=10 << 20, transcendentals=0),
        )(meta, block_order, w_near, code, e, *f_all, w if own_half else out)
        if own_half:
            out, w_near = result
        else:
            (out,) = result
    return jnp.transpose(out, (1, 0, 2))


def solution(mesh):
    in_specs = (P("rows", None, "cols"), P("rows", None, "cols"), P(), P("rows", None), P())
    out_specs = P("rows", None, "cols")
    return jax.shard_map(body, mesh=mesh, in_specs=in_specs, out_specs=out_specs, check_vma=False)
```
